128 devices in a mesh: seq: 16 (over x_lo, z, core), tensor: 8 (over y, x_hi).
Axes of the slice: x: 4 (x_hi: 2, x_lo: 2; x = x_hi * 2 + x_lo), y: 4, z: 4, core: 2. Of those that a mesh axis runs over, the one named last changes fastest.
Arguments:
- tokens: bfloat16 [2048, 8192], P('seq', 'tensor'), may hold values from -2000 to 2000
- cotangent: bfloat16 [2048, 8192], P('seq', 'tensor'), may hold values from -6 to 6
- gain: float32 [8192], P('tensor'), may hold values from 0.25 to 1.75
- w_gate: bfloat16 [8192, 14336], P('tensor', 'seq'), may hold values from -0.0625 to 0.0625
- w_up: bfloat16 [8192, 14336], P('tensor', 'seq'), may hold values from -0.0625 to 0.0625
- w_down: bfloat16 [14336, 8192], P('seq', 'tensor'), may hold values from -0.046875 to 0.046875
- probe: bfloat16 [8192, 14336], P('tensor', 'seq'), may hold values from -1 to 1, as said below
Outputs:
- hessian_probe: float32 [8192, 14336], P('tensor', 'seq')
The draws below stay inside these ranges and needn't reach their ends.
Inputs may be any that keep to these rules, and one draw needn't show every extreme that they name: `probe`: every entry is +1 or -1.
All inputs are finite; a program needn't handle non-finite values.
Results may differ from the reference program's by a relative error of at most 0.024.
Values may be sent and summed in bfloat16 or wider, within the bound.
No kernel may reach another device: no remote copies, remote signals or barrier semaphores. Data moves between devices by JAX's collectives and lax.ppermute only.
A program may use at most 128 MiB of HBM per device.

```python
import math
import jax
import jax.numpy as jnp
from jax import lax

D = 8192
FF = 14336
TOKENS = 2048
N_TENSOR = 8


def draw_tokens(key, part):
    base_key, row_key, column_key = jax.random.split(key, 3)
    position = jnp.arange(D, dtype=jnp.float32) / (D - 1)
    column_rough = jnp.exp(jax.random.uniform(column_key, (1, D), jnp.float32, 0.0, math.log(3.0)))
    random_part = jax.random.normal(base_key, (TOKENS, D), jnp.float32)
    row_scale = jnp.exp(jax.random.uniform(row_key, (TOKENS, 1), jnp.float32, 0.0, math.log(10.0)))
    column_trend = jnp.exp(position * math.log(4.0))[None, :]
    values = random_part * row_scale * column_trend * column_rough
    return jnp.clip(values, -2000.0, 2000.0).astype(jnp.bfloat16)


def draw_probe(key, part):
    coin_flips = jax.random.randint(key, (D, FF), 0, 2)
    return (2.0 * coin_flips.astype(jnp.float32) - 1.0).astype(jnp.bfloat16)


def shard_levels(own_key, shape, cuts, low, largest):
    def one(dim, shards_of):
        steps = jax.random.uniform(jax.random.fold_in(jax.random.fold_in(own_key, 6), dim), (shards_of,), jnp.float32, low / len(cuts), largest / len(cuts))
        return jnp.repeat(jnp.exp(steps), shape[dim] // shards_of).reshape((-1,) + (1,) * (len(shape) - dim - 1))

    factor_of = one(*cuts[0])
    for cut in cuts[1:]:
        factor_of = factor_of * one(*cut)
    return factor_of


def centred(rng, shape, scale, limit, cuts=(), kind=jnp.bfloat16):
    entries = jax.random.normal(rng, shape, jnp.float32) * scale
    if len(cuts) > 0:
        entries = shard_levels(rng, shape, cuts, -0.22, 0.18) * entries
    return jnp.clip(entries, min=-limit, max=limit).astype(kind)


def setup_inputs(seed: int = 0) -> dict:
    seeds = jax.random.split(jax.random.key(seed), 8)
    return {
        "tokens": draw_tokens(jax.random.fold_in(seeds[7], 71), 0),
        "cotangent": centred(seeds[1], (TOKENS, D), 1.0, 6.0, ((0, 16), (1, 8))),
        "gain": jnp.clip(1.0 + 0.15 * jax.random.normal(seeds[2], (D,), jnp.float32), 0.25, 1.75),
        "w_gate": centred(seeds[3], (D, FF), D ** -0.5, 0.0625, ((0, 8), (1, 16))),
        "w_up": centred(seeds[4], (D, FF), D ** -0.5, 0.0625, ((0, 8), (1, 16))),
        "w_down": centred(seeds[5], (FF, D), FF ** -0.5, 0.046875, ((0, 16), (1, 8))),
        "probe": draw_probe(jax.random.fold_in(seeds[7], 71), 0),
    }


epsilon = 1e-05

def blocked_product(left, right, contract_right):
    block_width = D // N_TENSOR

    def advance(running, block_index):
        offset = block_index * block_width
        left_block = lax.dynamic_slice_in_dim(left, offset, block_width, 1)
        right_block = lax.dynamic_slice_in_dim(right, offset, block_width, contract_right)
        partial_sum = lax.dot_general(left_block, right_block, (((1,), (contract_right,)), ((), ())), preferred_element_type=jnp.float32)
        rounded = lax.optimization_barrier(partial_sum.astype(jnp.bfloat16))
        return (running + rounded.astype(jnp.float32), None)
    output_width = right.shape[1 - contract_right]
    start_value = jnp.zeros((left.shape[0], output_width), jnp.float32)
    result, _ = lax.scan(advance, start_value, jnp.arange(N_TENSOR, dtype=jnp.int32))
    return result

def second_factor(pre_gate, pre_up, tangent, upstream):
    sigmoid_gate = jax.nn.sigmoid(pre_gate)
    curvature = sigmoid_gate * (1.0 - sigmoid_gate) * (2.0 + pre_gate * (1.0 - 2.0 * sigmoid_gate))
    return (upstream * pre_up * curvature * tangent).astype(jnp.bfloat16)

def reference(tokens, cotangent, gain, w_gate, w_up, w_down, probe):
    values = tokens.astype(jnp.float32)
    inverse = lax.rsqrt(lax.optimization_barrier(jnp.sum(values * values, axis=1)) / D + epsilon)
    normed = (values * inverse[:, None] * gain[None, :]).astype(jnp.bfloat16)
    pre_gate = blocked_product(normed, w_gate, 0)
    pre_up = blocked_product(normed, w_up, 0)
    tangent = blocked_product(normed, probe, 0)
    upstream = blocked_product(cotangent, w_down, 1)
    second = second_factor(pre_gate, pre_up, tangent, upstream)
    product = lax.dot_general(normed, second, (((0,), (0,)), ((), ())), preferred_element_type=jnp.float32)
    return product / TOKENS
```

```python
import jax
import jax.numpy as jnp
from jax import lax
from jax.sharding import PartitionSpec as P

D = 8192


epsilon = 1e-05


def second_factor(pre_gate, pre_up, tangent, upstream):
    sigmoid_gate = jax.nn.sigmoid(pre_gate)
    curvature = sigmoid_gate * (1.0 - sigmoid_gate) * (2.0 + pre_gate * (1.0 - 2.0 * sigmoid_gate))
    return (upstream * pre_up * curvature * tangent).astype(jnp.bfloat16)


def body(tokens, cotangent, gain, w_gate, w_up, w_down, probe):
    upstream_rows = lax.all_gather(cotangent, "seq", axis=0, tiled=True)
    values = tokens.astype(jnp.float32)
    squares = lax.psum(jnp.sum(values * values, axis=1), "tensor")
    inverse = lax.rsqrt(squares / D + epsilon)
    normed_local = (values * inverse[:, None] * gain[None, :]).astype(jnp.bfloat16)
    normed = lax.all_gather(normed_local, "seq", axis=0, tiled=True)
    total_tokens = normed.shape[0]
    parts = [
        jnp.dot(normed, weight, preferred_element_type=jnp.float32).astype(jnp.bfloat16)
        for weight in (w_gate, w_up, probe)
    ]
    parts.append(
        lax.dot_general(
            upstream_rows, w_down, (((1,), (1,)), ((), ())), preferred_element_type=jnp.float32
        ).astype(jnp.bfloat16)
    )
    summed = [
        lax.psum_scatter(p, "tensor", scatter_dimension=0, tiled=True).astype(jnp.float32)
        for p in parts
    ]
    second = second_factor(*summed)
    product = lax.dot_general(
        normed,
        lax.all_gather(second, "tensor", axis=0, tiled=True),
        (((0,), (0,)), ((), ())),
        preferred_element_type=jnp.float32,
    )
    return product / total_tokens


def solution(mesh):
    return jax.shard_map(
        body,
        mesh=mesh,
        in_specs=(
            P("seq", "tensor"),
            P("seq", "tensor"),
            P("tensor"),
            P("tensor", "seq"),
            P("tensor", "seq"),
            P("seq", "tensor"),
            P("tensor", "seq"),
        ),
        out_specs=P("tensor", "seq"),
        check_vma=False,
    )
```

```python
import functools

import jax
import jax.numpy as jnp
from jax import lax
from jax.experimental import pallas as pl
from jax.experimental.pallas import tpu as pltpu
from jax.sharding import PartitionSpec as P

D = 8192
CHUNKS = 2

epsilon = 1e-05


def second_factor(pre_gate, pre_up, tangent, upstream):
    sigmoid_gate = jax.nn.sigmoid(pre_gate)
    curvature = sigmoid_gate * (1.0 - sigmoid_gate) * (2.0 + pre_gate * (1.0 - 2.0 * sigmoid_gate))
    return (upstream * pre_up * curvature * tangent).astype(jnp.bfloat16)


def products_kernel(n_ref, c_ref, wg_ref, wu_ref, pr_ref, wd_ref, o_ref):
    f = wg_ref.shape[1]
    n = n_ref[...]
    for p, w_ref in enumerate((wg_ref, wu_ref, pr_ref)):
        o_ref[0, :, p * f:(p + 1) * f] = jnp.dot(
            n, w_ref[...], preferred_element_type=jnp.float32
        ).astype(o_ref.dtype)
    o_ref[0, :, 3 * f:4 * f] = lax.dot_general(
        c_ref[...], wd_ref[...], (((1,), (1,)), ((), ())), preferred_element_type=jnp.float32
    ).astype(o_ref.dtype)


def products(normed, cot, w_gate, w_up, probe, w_down, blocks):
    rows, width = normed.shape
    f = w_gate.shape[1]
    tm = rows // blocks
    full = lambda shape: pl.BlockSpec(shape, lambda i: (0, 0))
    return pl.pallas_call(
        products_kernel,
        out_shape=jax.ShapeDtypeStruct((blocks, tm, 4 * f), jnp.bfloat16),
        grid=(blocks,),
        in_specs=[
            pl.BlockSpec((tm, width), lambda i: (i, 0)),
            pl.BlockSpec((tm, width), lambda i: (i, 0)),
            full(w_gate.shape),
            full(w_up.shape),
            full(probe.shape),
            full(w_down.shape),
        ],
        out_specs=pl.BlockSpec((1, tm, 4 * f), lambda i: (i, 0, 0)),
        compiler_params=pltpu.CompilerParams(vmem_limit_bytes=48 * 1024 * 1024),
        cost_estimate=pl.CostEstimate(
            flops=2 * rows * width * f * 4,
            transcendentals=0,
            bytes_accessed=2 * (2 * rows * width + 4 * width * f + rows * 4 * f),
        ),
    )(normed, cot, w_gate, w_up, probe, w_down)


def body(tokens, cotangent, gain, w_gate, w_up, w_down, probe):
    n_tensor = lax.axis_size("tensor")
    values = tokens.astype(jnp.float32)
    squares = lax.psum(jnp.sum(values * values, axis=1), "tensor")
    inverse = lax.rsqrt(squares / D + epsilon)
    normed_local = (values * inverse[:, None] * gain[None, :]).astype(jnp.bfloat16)
    local_rows = tokens.shape[0]
    step = local_rows // CHUNKS
    unit_count = w_gate.shape[1]
    total = None
    total_tokens = 0
    for c in range(CHUNKS):
        rows = slice(c * step, (c + 1) * step)
        cot_c = lax.all_gather(cotangent[rows], "seq", axis=0, tiled=True)
        normed_c = lax.all_gather(normed_local[rows], "seq", axis=0, tiled=True)
        total_tokens += normed_c.shape[0]
        parts = products(normed_c, cot_c, w_gate, w_up, probe, w_down, n_tensor)
        received = lax.all_to_all(parts, "tensor", 0, 0, tiled=True)
        summed = jnp.sum(received.astype(jnp.float32), axis=0)
        second = second_factor(
            summed[:, :unit_count],
            summed[:, unit_count : 2 * unit_count],
            summed[:, 2 * unit_count : 3 * unit_count],
            summed[:, 3 * unit_count :],
        )
        piece = lax.dot_general(
            normed_c,
            lax.all_gather(second, "tensor", axis=0, tiled=True),
            (((0,), (0,)), ((), ())),
            preferred_element_type=jnp.float32,
        )
        total = piece if total is None else total + piece
    return total / total_tokens


def solution(mesh):
    return jax.shard_map(
        body,
        mesh=mesh,
        in_specs=(
            P("seq", "tensor"),
            P("seq", "tensor"),
            P("tensor"),
            P("tensor", "seq"),
            P("tensor", "seq"),
            P("seq", "tensor"),
            P("tensor", "seq"),
        ),
        out_specs=P("tensor", "seq"),
        check_vma=False,
    )
```

```python
import functools

import jax
import jax.numpy as jnp
from jax import lax
from jax.experimental import pallas as pl
from jax.experimental.pallas import tpu as pltpu
from jax.sharding import PartitionSpec as P

D = 8192

epsilon = 1e-05


def second_factor(pre_gate, pre_up, tangent, upstream):
    sigmoid_gate = jax.nn.sigmoid(pre_gate)
    curvature = sigmoid_gate * (1.0 - sigmoid_gate) * (2.0 + pre_gate * (1.0 - 2.0 * sigmoid_gate))
    return (upstream * pre_up * curvature * tangent).astype(jnp.bfloat16)


def products_kernel(n_ref, c_ref, wg_ref, wu_ref, pr_ref, wd_ref, o_ref):
    f = wg_ref.shape[1]
    n = n_ref[...]
    for p, w_ref in enumerate((wg_ref, wu_ref, pr_ref)):
        o_ref[0, :, p * f:(p + 1) * f] = jnp.dot(
            n, w_ref[...], preferred_element_type=jnp.float32
        ).astype(o_ref.dtype)
    o_ref[0, :, 3 * f:4 * f] = lax.dot_general(
        c_ref[...], wd_ref[...], (((1,), (1,)), ((), ())), preferred_element_type=jnp.float32
    ).astype(o_ref.dtype)


def products(normed, cot, w_gate, w_up, probe, w_down, blocks):
    rows, width = normed.shape
    f = w_gate.shape[1]
    tm = rows // blocks
    full = lambda shape: pl.BlockSpec(shape, lambda i: (0, 0))
    return pl.pallas_call(
        products_kernel,
        out_shape=jax.ShapeDtypeStruct((blocks, tm, 4 * f), jnp.bfloat16),
        grid=(blocks,),
        in_specs=[
            pl.BlockSpec((tm, width), lambda i: (i, 0)),
            pl.BlockSpec((tm, width), lambda i: (i, 0)),
            full(w_gate.shape),
            full(w_up.shape),
            full(probe.shape),
            full(w_down.shape),
        ],
        out_specs=pl.BlockSpec((1, tm, 4 * f), lambda i: (i, 0, 0)),
        compiler_params=pltpu.CompilerParams(vmem_limit_bytes=48 * 1024 * 1024),
        cost_estimate=pl.CostEstimate(
            flops=2 * rows * width * f * 4,
            transcendentals=0,
            bytes_accessed=2 * (2 * rows * width + 4 * width * f + rows * 4 * f),
        ),
    )(normed, cot, w_gate, w_up, probe, w_down)


def butterfly_sum(x, axis):
    n = lax.axis_size(axis)
    bit = 1
    while bit < n:
        x = x + lax.ppermute(x, axis, [(i, i ^ bit) for i in range(n)])
        bit *= 2
    return x


def body(tokens, cotangent, gain, w_gate, w_up, w_down, probe):
    n_tensor = lax.axis_size("tensor")
    width = tokens.shape[1]
    both = lax.all_gather(jnp.concatenate([tokens, cotangent], axis=1), "seq", axis=0, tiled=True)
    gathered = both[:, :width]
    upstream_rows = both[:, width:]
    values = gathered.astype(jnp.float32)
    squares = butterfly_sum(jnp.sum(values * values, axis=1), "tensor")
    inverse = lax.rsqrt(squares / D + epsilon)
    normed = (values * inverse[:, None] * gain[None, :]).astype(jnp.bfloat16)
    total_tokens = normed.shape[0]
    unit_count = w_gate.shape[1]
    parts = products(normed, upstream_rows, w_gate, w_up, probe, w_down, n_tensor)
    summed = lax.psum_scatter(parts, "tensor", scatter_dimension=0, tiled=True)[0].astype(jnp.float32)
    second = second_factor(
        summed[:, :unit_count],
        summed[:, unit_count : 2 * unit_count],
        summed[:, 2 * unit_count : 3 * unit_count],
        summed[:, 3 * unit_count :],
    )
    product = lax.dot_general(
        normed,
        lax.all_gather(second, "tensor", axis=0, tiled=True),
        (((0,), (0,)), ((), ())),
        preferred_element_type=jnp.float32,
    )
    return product / total_tokens


def solution(mesh):
    return jax.shard_map(
        body,
        mesh=mesh,
        in_specs=(
            P("seq", "tensor"),
            P("seq", "tensor"),
            P("tensor"),
            P("tensor", "seq"),
            P("tensor", "seq"),
            P("seq", "tensor"),
            P("tensor", "seq"),
        ),
        out_specs=P("tensor", "seq"),
        check_vma=False,
    )
```

```python
import functools

import jax
import jax.numpy as jnp
from jax import lax
from jax.experimental import pallas as pl
from jax.experimental.pallas import tpu as pltpu
from jax.sharding import PartitionSpec as P

D = 8192

epsilon = 1e-05


def second_factor(pre_gate, pre_up, tangent, upstream):
    sigmoid_gate = jax.nn.sigmoid(pre_gate)
    curvature = sigmoid_gate * (1.0 - sigmoid_gate) * (2.0 + pre_gate * (1.0 - 2.0 * sigmoid_gate))
    return (upstream * pre_up * curvature * tangent).astype(jnp.bfloat16)


def products_kernel(n_ref, c_ref, wg_ref, wu_ref, pr_ref, wd_ref, o_ref):
    f = wg_ref.shape[1]
    n = n_ref[...]
    for p, w_ref in enumerate((wg_ref, wu_ref, pr_ref)):
        o_ref[0, :, p * f:(p + 1) * f] = jnp.dot(
            n, w_ref[...], preferred_element_type=jnp.float32
        ).astype(o_ref.dtype)
    o_ref[0, :, 3 * f:4 * f] = lax.dot_general(
        c_ref[...], wd_ref[...], (((1,), (1,)), ((), ())), preferred_element_type=jnp.float32
    ).astype(o_ref.dtype)


def products(both, w_gate, w_up, probe, w_down, blocks):
    rows, width = both.shape[0], both.shape[1] // 2
    f = w_gate.shape[1]
    tm = rows // blocks
    full = lambda shape: pl.BlockSpec(shape, lambda i: (0, 0))
    return pl.pallas_call(
        products_kernel,
        out_shape=jax.ShapeDtypeStruct((blocks, tm, 4 * f), jnp.bfloat16),
        grid=(blocks,),
        in_specs=[
            pl.BlockSpec((tm, width), lambda i: (i, 0)),
            pl.BlockSpec((tm, width), lambda i: (i, 1)),
            full(w_gate.shape),
            full(w_up.shape),
            full(probe.shape),
            full(w_down.shape),
        ],
        out_specs=pl.BlockSpec((1, tm, 4 * f), lambda i: (i, 0, 0)),
        compiler_params=pltpu.CompilerParams(vmem_limit_bytes=48 * 1024 * 1024),
        cost_estimate=pl.CostEstimate(
            flops=2 * rows * width * f * 4,
            transcendentals=0,
            bytes_accessed=2 * (2 * rows * width + 4 * width * f + rows * 4 * f),
        ),
    )(both, both, w_gate, w_up, probe, w_down)


def gather_tensor(x, axis):
    n = lax.axis_size(axis)
    repeated = jnp.broadcast_to(x[None], (n,) + x.shape)
    got = lax.all_to_all(repeated, axis, 0, 0, tiled=True)
    return got.reshape((n * x.shape[0],) + x.shape[1:])


def butterfly_sum(x, axis):
    n = lax.axis_size(axis)
    bit = 1
    while bit < n:
        x = x + lax.ppermute(x, axis, [(i, i ^ bit) for i in range(n)])
        bit *= 2
    return x


def body(tokens, cotangent, gain, w_gate, w_up, w_down, probe):
    n_tensor = lax.axis_size("tensor")
    width = tokens.shape[1]
    values = tokens.astype(jnp.float32)
    squares = butterfly_sum(jnp.sum(values * values, axis=1), "tensor")
    inverse = lax.rsqrt(squares / D + epsilon)
    normed_local = (values * inverse[:, None] * gain[None, :]).astype(jnp.bfloat16)
    both = lax.all_gather(jnp.concatenate([normed_local, cotangent], axis=1), "seq", axis=0, tiled=True)
    total_tokens = both.shape[0]
    unit_count = w_gate.shape[1]
    parts = products(both, w_gate, w_up, probe, w_down, n_tensor)
    summed = lax.psum_scatter(parts, "tensor", scatter_dimension=0, tiled=True)[0].astype(jnp.float32)
    second = second_factor(
        summed[:, :unit_count],
        summed[:, unit_count : 2 * unit_count],
        summed[:, 2 * unit_count : 3 * unit_count],
        summed[:, 3 * unit_count :],
    )
    product = lax.dot_general(
        both[:, :width],
        gather_tensor(second, "tensor"),
        (((0,), (0,)), ((), ())),
        preferred_element_type=jnp.float32,
    )
    return product / total_tokens


def solution(mesh):
    return jax.shard_map(
        body,
        mesh=mesh,
        in_specs=(
            P("seq", "tensor"),
            P("seq", "tensor"),
            P("tensor"),
            P("tensor", "seq"),
            P("tensor", "seq"),
            P("seq", "tensor"),
            P("tensor", "seq"),
        ),
        out_specs=P("tensor", "seq"),
        check_vma=False,
    )
```

```python
import functools

import jax
import jax.numpy as jnp
from jax import lax
from jax.experimental import pallas as pl
from jax.experimental.pallas import tpu as pltpu
from jax.sharding import PartitionSpec as P

D = 8192

epsilon = 1e-05


def second_factor(pre_gate, pre_up, tangent, upstream):
    sigmoid_gate = jax.nn.sigmoid(pre_gate)
    curvature = sigmoid_gate * (1.0 - sigmoid_gate) * (2.0 + pre_gate * (1.0 - 2.0 * sigmoid_gate))
    return (upstream * pre_up * curvature * tangent).astype(jnp.bfloat16)


def products_kernel(n_ref, c_ref, *refs, pairs):
    o_ref = refs[-1]
    for p, (use_cot, w_ref) in enumerate(zip(pairs, refs[:-1])):
        f = w_ref.shape[0] if use_cot else w_ref.shape[1]
        if use_cot:
            value = lax.dot_general(
                c_ref[...], w_ref[...], (((1,), (1,)), ((), ())), preferred_element_type=jnp.float32
            )
        else:
            value = jnp.dot(n_ref[...], w_ref[...], preferred_element_type=jnp.float32)
        o_ref[0, :, p * f:(p + 1) * f] = value.astype(o_ref.dtype)


def products(both, weights, pairs, blocks):
    rows, width = both.shape[0], both.shape[1] // 2
    f = weights[0].shape[0] if pairs[0] else weights[0].shape[1]
    tm = rows // blocks
    full = lambda shape: pl.BlockSpec(shape, lambda i: (0, 0))
    count = len(weights)
    return pl.pallas_call(
        functools.partial(products_kernel, pairs=tuple(pairs)),
        out_shape=jax.ShapeDtypeStruct((blocks, tm, count * f), jnp.bfloat16),
        grid=(blocks,),
        in_specs=[
            pl.BlockSpec((tm, width), lambda i: (i, 0)),
            pl.BlockSpec((tm, width), lambda i: (i, 1)),
        ] + [full(w.shape) for w in weights],
        out_specs=pl.BlockSpec((1, tm, count * f), lambda i: (i, 0, 0)),
        compiler_params=pltpu.CompilerParams(vmem_limit_bytes=48 * 1024 * 1024),
        cost_estimate=pl.CostEstimate(
            flops=2 * rows * width * f * count,
            transcendentals=0,
            bytes_accessed=2 * (2 * rows * width + count * width * f + rows * count * f),
        ),
    )(both, both, *weights)


def gather_tensor(x, axis):
    n = lax.axis_size(axis)
    repeated = jnp.broadcast_to(x[None], (n,) + x.shape)
    got = lax.all_to_all(repeated, axis, 0, 0, tiled=True)
    return got.reshape((n * x.shape[0],) + x.shape[1:])


def butterfly_sum(x, axis):
    n = lax.axis_size(axis)
    bit = 1
    while bit < n:
        x = x + lax.ppermute(x, axis, [(i, i ^ bit) for i in range(n)])
        bit *= 2
    return x


def body(tokens, cotangent, gain, w_gate, w_up, w_down, probe):
    n_tensor = lax.axis_size("tensor")
    width = tokens.shape[1]
    values = tokens.astype(jnp.float32)
    squares = butterfly_sum(jnp.sum(values * values, axis=1), "tensor")
    inverse = lax.rsqrt(squares / D + epsilon)
    normed_local = (values * inverse[:, None] * gain[None, :]).astype(jnp.bfloat16)
    both = lax.all_gather(jnp.concatenate([normed_local, cotangent], axis=1), "seq", axis=0, tiled=True)
    total_tokens = both.shape[0]
    unit_count = w_gate.shape[1]
    first = products(both, (w_down, w_up), (True, False), n_tensor)
    received = lax.all_to_all(first, "tensor", 0, 0, tiled=True)
    rest = products(both, (w_gate, probe), (False, False), n_tensor)
    scattered = lax.psum_scatter(rest, "tensor", scatter_dimension=0, tiled=True)[0].astype(jnp.float32)
    summed = jnp.sum(received.astype(jnp.float32), axis=0)
    second = second_factor(
        scattered[:, :unit_count],
        summed[:, unit_count:],
        scattered[:, unit_count:],
        summed[:, :unit_count],
    )
    product = lax.dot_general(
        both[:, :width],
        gather_tensor(second, "tensor"),
        (((0,), (0,)), ((), ())),
        preferred_element_type=jnp.float32,
    )
    return product / total_tokens


def solution(mesh):
    return jax.shard_map(
        body,
        mesh=mesh,
        in_specs=(
            P("seq", "tensor"),
            P("seq", "tensor"),
            P("tensor"),
            P("tensor", "seq"),
            P("tensor", "seq"),
            P("seq", "tensor"),
            P("tensor", "seq"),
        ),
        out_specs=P("tensor", "seq"),
        check_vma=False,
    )
```

```python
import functools

import jax
import jax.numpy as jnp
from jax import lax
from jax.experimental import pallas as pl
from jax.experimental.pallas import tpu as pltpu
from jax.sharding import PartitionSpec as P

D = 8192

epsilon = 1e-05


def second_factor(pre_gate, pre_up, tangent, upstream):
    sigmoid_gate = jax.nn.sigmoid(pre_gate)
    curvature = sigmoid_gate * (1.0 - sigmoid_gate) * (2.0 + pre_gate * (1.0 - 2.0 * sigmoid_gate))
    return (upstream * pre_up * curvature * tangent).astype(jnp.bfloat16)


def products_kernel(t_ref, c_ref, inv_ref, gain_ref, wg_ref, wu_ref, pr_ref, wd_ref, o_ref, n_out_ref):
    f = wg_ref.shape[1]
    n = (t_ref[...].astype(jnp.float32) * inv_ref[...] * gain_ref[...]).astype(jnp.bfloat16)
    n_out_ref[...] = n
    for p, w_ref in enumerate((wg_ref, wu_ref, pr_ref)):
        o_ref[0, :, p * f:(p + 1) * f] = jnp.dot(
            n, w_ref[...], preferred_element_type=jnp.float32
        ).astype(o_ref.dtype)
    o_ref[0, :, 3 * f:4 * f] = lax.dot_general(
        c_ref[...], wd_ref[...], (((1,), (1,)), ((), ())), preferred_element_type=jnp.float32
    ).astype(o_ref.dtype)


def products(both, inverse, gain, w_gate, w_up, probe, w_down, blocks):
    rows, width = both.shape[0], both.shape[1] // 2
    f = w_gate.shape[1]
    tm = rows // blocks
    full = lambda shape: pl.BlockSpec(shape, lambda i: (0, 0))
    return pl.pallas_call(
        products_kernel,
        out_shape=(
            jax.ShapeDtypeStruct((blocks, tm, 4 * f), jnp.bfloat16),
            jax.ShapeDtypeStruct((rows, width), jnp.bfloat16),
        ),
        grid=(blocks,),
        in_specs=[
            pl.BlockSpec((tm, width), lambda i: (i, 0)),
            pl.BlockSpec((tm, width), lambda i: (i, 1)),
            pl.BlockSpec((tm, 1), lambda i: (i, 0)),
            full((1, width)),
            full(w_gate.shape),
            full(w_up.shape),
            full(probe.shape),
            full(w_down.shape),
        ],
        out_specs=(
            pl.BlockSpec((1, tm, 4 * f), lambda i: (i, 0, 0)),
            pl.BlockSpec((tm, width), lambda i: (i, 0)),
        ),
        compiler_params=pltpu.CompilerParams(vmem_limit_bytes=48 * 1024 * 1024),
        cost_estimate=pl.CostEstimate(
            flops=2 * rows * width * f * 4,
            transcendentals=0,
            bytes_accessed=2 * (3 * rows * width + 4 * width * f + rows * 4 * f),
        ),
    )(both, both, inverse.reshape(rows, 1), gain.reshape(1, width), w_gate, w_up, probe, w_down)


def gather_tensor(x, axis):
    n = lax.axis_size(axis)
    repeated = jnp.broadcast_to(x[None], (n,) + x.shape)
    got = lax.all_to_all(repeated, axis, 0, 0, tiled=True)
    return got.reshape((n * x.shape[0],) + x.shape[1:])


def butterfly_sum(x, axis):
    n = lax.axis_size(axis)
    bit = 1
    while bit < n:
        x = x + lax.ppermute(x, axis, [(i, i ^ bit) for i in range(n)])
        bit *= 2
    return x


def body(tokens, cotangent, gain, w_gate, w_up, w_down, probe):
    n_tensor = lax.axis_size("tensor")
    width = tokens.shape[1]
    both = lax.all_gather(jnp.concatenate([tokens, cotangent], axis=1), "seq", axis=0, tiled=True)
    values = tokens.astype(jnp.float32)
    squares = butterfly_sum(jnp.sum(values * values, axis=1), "tensor")
    inverse = gather_tensor(lax.rsqrt(squares / D + epsilon), "seq")
    total_tokens = both.shape[0]
    unit_count = w_gate.shape[1]
    parts, normed = products(both, inverse, gain, w_gate, w_up, probe, w_down, n_tensor)
    summed = lax.psum_scatter(parts, "tensor", scatter_dimension=0, tiled=True)[0].astype(jnp.float32)
    second = second_factor(
        summed[:, :unit_count],
        summed[:, unit_count : 2 * unit_count],
        summed[:, 2 * unit_count : 3 * unit_count],
        summed[:, 3 * unit_count :],
    )
    product = lax.dot_general(
        normed,
        gather_tensor(second, "tensor"),
        (((0,), (0,)), ((), ())),
        preferred_element_type=jnp.float32,
    )
    return product / total_tokens


def solution(mesh):
    return jax.shard_map(
        body,
        mesh=mesh,
        in_specs=(
            P("seq", "tensor"),
            P("seq", "tensor"),
            P("tensor"),
            P("tensor", "seq"),
            P("tensor", "seq"),
            P("seq", "tensor"),
            P("tensor", "seq"),
        ),
        out_specs=P("tensor", "seq"),
        check_vma=False,
    )
```

```python
import jax
import jax.numpy as jnp
from jax import lax
from jax.experimental import pallas as pl
from jax.experimental.pallas import tpu as pltpu
from jax.sharding import Mesh, PartitionSpec as P


D = 8192

epsilon = 1e-05


def second_factor(pre_gate, pre_up, tangent, upstream):
    sigmoid_gate = jax.nn.sigmoid(pre_gate)
    curvature = sigmoid_gate * (1.0 - sigmoid_gate) * (2.0 + pre_gate * (1.0 - 2.0 * sigmoid_gate))
    return (upstream * pre_up * curvature * tangent).astype(jnp.bfloat16)


def products_kernel(t_ref, c_ref, inv_ref, gain_ref, wg_ref, wu_ref, pr_ref, wd_ref, o_ref, n_out_ref):
    f = wg_ref.shape[1]
    n = (t_ref[...].astype(jnp.float32) * inv_ref[...] * gain_ref[...]).astype(jnp.bfloat16)
    n_out_ref[...] = n
    for p, w_ref in enumerate((wg_ref, wu_ref, pr_ref)):
        o_ref[0, :, p * f:(p + 1) * f] = jnp.dot(
            n, w_ref[...], preferred_element_type=jnp.float32
        ).astype(o_ref.dtype)
    o_ref[0, :, 3 * f:4 * f] = lax.dot_general(
        c_ref[...], wd_ref[...], (((1,), (1,)), ((), ())), preferred_element_type=jnp.float32
    ).astype(o_ref.dtype)


def products(both, inverse, gain, w_gate, w_up, probe, w_down, blocks):
    rows, width = both.shape[0], both.shape[1] // 2
    f = w_gate.shape[1]
    tm = rows // blocks
    full = lambda shape: pl.BlockSpec(shape, lambda i: (0, 0))
    return pl.pallas_call(
        products_kernel,
        out_shape=(
            jax.ShapeDtypeStruct((blocks, tm, 4 * f), jnp.bfloat16),
            jax.ShapeDtypeStruct((rows, width), jnp.bfloat16),
        ),
        grid=(blocks,),
        in_specs=[
            pl.BlockSpec((tm, width), lambda i: (i, 0)),
            pl.BlockSpec((tm, width), lambda i: (i, 1)),
            pl.BlockSpec((tm, 1), lambda i: (i, 0)),
            full((1, width)),
            full(w_gate.shape),
            full(w_up.shape),
            full(probe.shape),
            full(w_down.shape),
        ],
        out_specs=(
            pl.BlockSpec((1, tm, 4 * f), lambda i: (i, 0, 0)),
            pl.BlockSpec((tm, width), lambda i: (i, 0)),
        ),
        compiler_params=pltpu.CompilerParams(vmem_limit_bytes=48 * 1024 * 1024),
        cost_estimate=pl.CostEstimate(
            flops=2 * rows * width * f * 4,
            transcendentals=0,
            bytes_accessed=2 * (3 * rows * width + 4 * width * f + rows * 4 * f),
        ),
    )(both, both, inverse.reshape(rows, 1), gain.reshape(1, width), w_gate, w_up, probe, w_down)


def gather_tensor(x, axis):
    n = lax.axis_size(axis)
    repeated = jnp.broadcast_to(x[None], (n,) + x.shape)
    got = lax.all_to_all(repeated, axis, 0, 0, tiled=True)
    return got.reshape((n * x.shape[0],) + x.shape[1:])


def butterfly_sum(x, axis):
    n = lax.axis_size(axis)
    bit = 1
    while bit < n:
        x = x + lax.ppermute(x, axis, [(i, i ^ bit) for i in range(n)])
        bit *= 2
    return x


SEQ = ("xl", "z", "c")
TEN = ("y", "xh")


def body(tokens, cotangent, gain, w_gate, w_up, w_down, probe):
    n_tensor = lax.axis_size(TEN)
    local_rows = tokens.shape[0]
    core = lax.axis_index("c")
    own = lax.all_gather(jnp.concatenate([tokens, cotangent], axis=1), ("xl", "z"), axis=0, tiled=True)
    other = lax.ppermute(own, "c", [(0, 1), (1, 0)])
    both = jnp.concatenate([own, other], axis=0)
    values = tokens.astype(jnp.float32)
    squares = butterfly_sum(jnp.sum(values * values, axis=1), TEN)
    inverse = gather_tensor(lax.rsqrt(squares / D + epsilon), SEQ).reshape(-1, 2, local_rows)
    inverse = jnp.concatenate(
        [lax.dynamic_index_in_dim(inverse, core, 1, keepdims=False),
         lax.dynamic_index_in_dim(inverse, 1 - core, 1, keepdims=False)], axis=0
    ).reshape(-1)
    total_tokens = both.shape[0]
    unit_count = w_gate.shape[1]
    parts, normed = products(both, inverse, gain, w_gate, w_up, probe, w_down, n_tensor)
    summed = lax.psum_scatter(parts, TEN, scatter_dimension=0, tiled=True)[0].astype(jnp.float32)
    second = second_factor(
        summed[:, :unit_count],
        summed[:, unit_count : 2 * unit_count],
        summed[:, 2 * unit_count : 3 * unit_count],
        summed[:, 3 * unit_count :],
    )
    product = lax.dot_general(
        normed,
        gather_tensor(second, TEN),
        (((0,), (0,)), ((), ())),
        preferred_element_type=jnp.float32,
    )
    return product / total_tokens


def solution(mesh):
    seq_size, tensor_size = mesh.devices.shape
    mesh5 = Mesh(
        mesh.devices.reshape(seq_size // 8, 4, 2, tensor_size // 2, 2), SEQ + TEN
    )
    return jax.shard_map(
        body,
        mesh=mesh5,
        in_specs=(
            P(SEQ, TEN),
            P(SEQ, TEN),
            P(TEN),
            P(TEN, SEQ),
            P(TEN, SEQ),
            P(SEQ, TEN),
            P(TEN, SEQ),
        ),
        out_specs=P(TEN, SEQ),
        check_vma=False,
    )
```

```python
import functools

import jax
import jax.numpy as jnp
from jax import lax
from jax.experimental import pallas as pl
from jax.experimental.pallas import tpu as pltpu
from jax.sharding import PartitionSpec as P

D = 8192

epsilon = 1e-05


def second_factor(pre_gate, pre_up, tangent, upstream):
    sigmoid_gate = jax.nn.sigmoid(pre_gate)
    curvature = sigmoid_gate * (1.0 - sigmoid_gate) * (2.0 + pre_gate * (1.0 - 2.0 * sigmoid_gate))
    return (upstream * pre_up * curvature * tangent).astype(jnp.bfloat16)


def products_kernel(t_ref, c_ref, inv_ref, gain_ref, wg_hbm, wu_hbm, pr_hbm, wd_hbm, o_ref, n_out_ref,
                    wg_ref, wu_ref, pr_ref, wd_ref, sems):
    first = pl.program_id(0) == 0
    copies = [
        pltpu.make_async_copy(src, dst, sems.at[k])
        for k, (src, dst) in enumerate(
            ((wg_hbm, wg_ref), (wu_hbm, wu_ref), (pr_hbm, pr_ref), (wd_hbm, wd_ref))
        )
    ]

    @pl.when(first)
    def _():
        for copy in copies:
            copy.start()

    f = wg_ref.shape[1]
    n = (t_ref[...].astype(jnp.float32) * inv_ref[...] * gain_ref[...]).astype(jnp.bfloat16)
    n_out_ref[...] = n
    for p, w_ref in enumerate((wg_ref, wu_ref, pr_ref)):
        @pl.when(first)
        def _():
            copies[p].wait()

        o_ref[0, :, p * f:(p + 1) * f] = jnp.dot(
            n, w_ref[...], preferred_element_type=jnp.float32
        ).astype(o_ref.dtype)

    @pl.when(first)
    def _():
        copies[3].wait()

    o_ref[0, :, 3 * f:4 * f] = lax.dot_general(
        c_ref[...], wd_ref[...], (((1,), (1,)), ((), ())), preferred_element_type=jnp.float32
    ).astype(o_ref.dtype)


def products(both, inverse, gain, w_gate, w_up, probe, w_down, blocks):
    rows, width = both.shape[0], both.shape[1] // 2
    f = w_gate.shape[1]
    tm = rows // blocks
    hbm = pl.BlockSpec(memory_space=pltpu.HBM)
    return pl.pallas_call(
        products_kernel,
        out_shape=(
            jax.ShapeDtypeStruct((blocks, tm, 4 * f), jnp.bfloat16),
            jax.ShapeDtypeStruct((rows, width), jnp.bfloat16),
        ),
        grid=(blocks,),
        in_specs=[
            pl.BlockSpec((tm, width), lambda i: (i, 0)),
            pl.BlockSpec((tm, width), lambda i: (i, 1)),
            pl.BlockSpec((tm, 1), lambda i: (i, 0)),
            pl.BlockSpec((1, width), lambda i: (0, 0)),
            hbm,
            hbm,
            hbm,
            hbm,
        ],
        out_specs=(
            pl.BlockSpec((1, tm, 4 * f), lambda i: (i, 0, 0)),
            pl.BlockSpec((tm, width), lambda i: (i, 0)),
        ),
        scratch_shapes=[
            pltpu.VMEM(w_gate.shape, w_gate.dtype),
            pltpu.VMEM(w_up.shape, w_up.dtype),
            pltpu.VMEM(probe.shape, probe.dtype),
            pltpu.VMEM(w_down.shape, w_down.dtype),
            pltpu.SemaphoreType.DMA((4,)),
        ],
        compiler_params=pltpu.CompilerParams(dimension_semantics=("arbitrary",)),
        cost_estimate=pl.CostEstimate(
            flops=2 * rows * width * f * 4,
            transcendentals=0,
            bytes_accessed=2 * (3 * rows * width + 4 * width * f + rows * 4 * f),
        ),
    )(both, both, inverse.reshape(rows, 1), gain.reshape(1, width), w_gate, w_up, probe, w_down)


def gather_tensor(x, axis):
    n = lax.axis_size(axis)
    repeated = jnp.broadcast_to(x[None], (n,) + x.shape)
    got = lax.all_to_all(repeated, axis, 0, 0, tiled=True)
    return got.reshape((n * x.shape[0],) + x.shape[1:])


def butterfly_sum(x, axis):
    n = lax.axis_size(axis)
    bit = 1
    while bit < n:
        x = x + lax.ppermute(x, axis, [(i, i ^ bit) for i in range(n)])
        bit *= 2
    return x


def body(tokens, cotangent, gain, w_gate, w_up, w_down, probe):
    n_tensor = lax.axis_size("tensor")
    width = tokens.shape[1]
    both = lax.all_gather(jnp.concatenate([tokens, cotangent], axis=1), "seq", axis=0, tiled=True)
    values = tokens.astype(jnp.float32)
    squares = butterfly_sum(jnp.sum(values * values, axis=1), "tensor")
    inverse = gather_tensor(lax.rsqrt(squares / D + epsilon), "seq")
    total_tokens = both.shape[0]
    unit_count = w_gate.shape[1]
    parts, normed = products(both, inverse, gain, w_gate, w_up, probe, w_down, n_tensor)
    summed = lax.psum_scatter(parts, "tensor", scatter_dimension=0, tiled=True)[0].astype(jnp.float32)
    second = second_factor(
        summed[:, :unit_count],
        summed[:, unit_count : 2 * unit_count],
        summed[:, 2 * unit_count : 3 * unit_count],
        summed[:, 3 * unit_count :],
    )
    product = lax.dot_general(
        normed,
        gather_tensor(second, "tensor"),
        (((0,), (0,)), ((), ())),
        preferred_element_type=jnp.float32,
    )
    return product / total_tokens


def solution(mesh):
    return jax.shard_map(
        body,
        mesh=mesh,
        in_specs=(
            P("seq", "tensor"),
            P("seq", "tensor"),
            P("tensor"),
            P("tensor", "seq"),
            P("tensor", "seq"),
            P("seq", "tensor"),
            P("tensor", "seq"),
        ),
        out_specs=P("tensor", "seq"),
        check_vma=False,
    )
```

```python
import functools

import jax
import jax.numpy as jnp
from jax import lax
from jax.experimental import pallas as pl
from jax.experimental.pallas import tpu as pltpu
from jax.sharding import PartitionSpec as P

D = 8192

epsilon = 1e-05


def second_factor(pre_gate, pre_up, tangent, upstream):
    sigmoid_gate = jax.nn.sigmoid(pre_gate)
    curvature = sigmoid_gate * (1.0 - sigmoid_gate) * (2.0 + pre_gate * (1.0 - 2.0 * sigmoid_gate))
    return (upstream * pre_up * curvature * tangent).astype(jnp.bfloat16)


def products_kernel(t_ref, c_ref, inv_ref, gain_ref, wg_ref, wu_ref, pr_ref, wd_ref, o_ref, n_out_ref):
    f = wg_ref.shape[1]
    split, part = o_ref.shape[0], o_ref.shape[1]
    n = (t_ref[...].astype(jnp.float32) * inv_ref[...] * gain_ref[...]).astype(jnp.bfloat16)
    n_out_ref[...] = n
    values = [jnp.dot(n, w_ref[...], preferred_element_type=jnp.float32) for w_ref in (wg_ref, wu_ref, pr_ref)]
    values.append(
        lax.dot_general(
            c_ref[...], wd_ref[...], (((1,), (1,)), ((), ())), preferred_element_type=jnp.float32
        )
    )
    for p, value in enumerate(values):
        for j in range(split):
            o_ref[j, :, p * f:(p + 1) * f] = value[j * part:(j + 1) * part].astype(o_ref.dtype)


def products(both, inverse, gain, w_gate, w_up, probe, w_down, blocks, split=2):
    rows, width = both.shape[0], both.shape[1] // 2
    f = w_gate.shape[1]
    part = rows // blocks
    tm = part * split
    full = lambda shape: pl.BlockSpec(shape, lambda i: (0, 0))
    return pl.pallas_call(
        products_kernel,
        out_shape=(
            jax.ShapeDtypeStruct((blocks, part, 4 * f), jnp.bfloat16),
            jax.ShapeDtypeStruct((rows, width), jnp.bfloat16),
        ),
        grid=(blocks // split,),
        in_specs=[
            pl.BlockSpec((tm, width), lambda i: (i, 0)),
            pl.BlockSpec((tm, width), lambda i: (i, 1)),
            pl.BlockSpec((tm, 1), lambda i: (i, 0)),
            full((1, width)),
            full(w_gate.shape),
            full(w_up.shape),
            full(probe.shape),
            full(w_down.shape),
        ],
        out_specs=(
            pl.BlockSpec((split, part, 4 * f), lambda i: (i, 0, 0)),
            pl.BlockSpec((tm, width), lambda i: (i, 0)),
        ),
        compiler_params=pltpu.CompilerParams(vmem_limit_bytes=48 * 1024 * 1024),
        cost_estimate=pl.CostEstimate(
            flops=2 * rows * width * f * 4,
            transcendentals=0,
            bytes_accessed=2 * (3 * rows * width + 4 * width * f + rows * 4 * f),
        ),
    )(both, both, inverse.reshape(rows, 1), gain.reshape(1, width), w_gate, w_up, probe, w_down)


def gather_tensor(x, axis):
    n = lax.axis_size(axis)
    repeated = jnp.broadcast_to(x[None], (n,) + x.shape)
    got = lax.all_to_all(repeated, axis, 0, 0, tiled=True)
    return got.reshape((n * x.shape[0],) + x.shape[1:])


def butterfly_sum(x, axis):
    n = lax.axis_size(axis)
    bit = 1
    while bit < n:
        x = x + lax.ppermute(x, axis, [(i, i ^ bit) for i in range(n)])
        bit *= 2
    return x


def body(tokens, cotangent, gain, w_gate, w_up, w_down, probe):
    n_tensor = lax.axis_size("tensor")
    width = tokens.shape[1]
    both = lax.all_gather(jnp.concatenate([tokens, cotangent], axis=1), "seq", axis=0, tiled=True)
    values = tokens.astype(jnp.float32)
    squares = butterfly_sum(jnp.sum(values * values, axis=1), "tensor")
    inverse = gather_tensor(lax.rsqrt(squares / D + epsilon), "seq")
    total_tokens = both.shape[0]
    unit_count = w_gate.shape[1]
    parts, normed = products(both, inverse, gain, w_gate, w_up, probe, w_down, n_tensor)
    summed = lax.psum_scatter(parts, "tensor", scatter_dimension=0, tiled=True)[0].astype(jnp.float32)
    second = second_factor(
        summed[:, :unit_count],
        summed[:, unit_count : 2 * unit_count],
        summed[:, 2 * unit_count : 3 * unit_count],
        summed[:, 3 * unit_count :],
    )
    product = lax.dot_general(
        normed,
        gather_tensor(second, "tensor"),
        (((0,), (0,)), ((), ())),
        preferred_element_type=jnp.float32,
    )
    return product / total_tokens


def solution(mesh):
    return jax.shard_map(
        body,
        mesh=mesh,
        in_specs=(
            P("seq", "tensor"),
            P("seq", "tensor"),
            P("tensor"),
            P("tensor", "seq"),
            P("tensor", "seq"),
            P("seq", "tensor"),
            P("tensor", "seq"),
        ),
        out_specs=P("tensor", "seq"),
        check_vma=False,
    )
```

```python
import functools

import jax
import jax.numpy as jnp
from jax import lax
from jax.experimental import pallas as pl
from jax.experimental.pallas import tpu as pltpu
from jax.sharding import PartitionSpec as P

D = 8192

epsilon = 1e-05


def second_factor(pre_gate, pre_up, tangent, upstream):
    sigmoid_gate = jax.nn.sigmoid(pre_gate)
    curvature = sigmoid_gate * (1.0 - sigmoid_gate) * (2.0 + pre_gate * (1.0 - 2.0 * sigmoid_gate))
    return (upstream * pre_up * curvature * tangent).astype(jnp.bfloat16)


def products_kernel(t_ref, c_ref, inv_ref, gain_ref, wg_ref, wu_ref, pr_ref, wd_ref, o_ref, n_out_ref):
    f = wg_ref.shape[1]
    n = (t_ref[...].astype(jnp.float32) * inv_ref[...] * gain_ref[...]).astype(jnp.bfloat16)
    n_out_ref[...] = n
    for p, w_ref in enumerate((wg_ref, wu_ref, pr_ref)):
        o_ref[0, :, p * f:(p + 1) * f] = jnp.dot(
            n, w_ref[...], preferred_element_type=jnp.float32
        ).astype(o_ref.dtype)
    o_ref[0, :, 3 * f:4 * f] = lax.dot_general(
        c_ref[...], wd_ref[...], (((1,), (1,)), ((), ())), preferred_element_type=jnp.float32
    ).astype(o_ref.dtype)


def products(both, inverse, gain, w_gate, w_up, probe, w_down, blocks):
    rows, width = both.shape[0], both.shape[1] // 2
    f = w_gate.shape[1]
    tm = rows // blocks
    full = lambda shape: pl.BlockSpec(shape, lambda i: (0, 0))
    return pl.pallas_call(
        products_kernel,
        out_shape=(
            jax.ShapeDtypeStruct((blocks, tm, 4 * f), jnp.bfloat16),
            jax.ShapeDtypeStruct((rows, width), jnp.bfloat16),
        ),
        grid=(blocks,),
        in_specs=[
            pl.BlockSpec((tm, width), lambda i: (i, 0)),
            pl.BlockSpec((tm, width), lambda i: (i, 1)),
            pl.BlockSpec((tm, 1), lambda i: (i, 0)),
            full((1, width)),
            full(w_gate.shape),
            full(w_up.shape),
            full(probe.shape),
            full(w_down.shape),
        ],
        out_specs=(
            pl.BlockSpec((1, tm, 4 * f), lambda i: (i, 0, 0)),
            pl.BlockSpec((tm, width), lambda i: (i, 0)),
        ),
        compiler_params=pltpu.CompilerParams(vmem_limit_bytes=48 * 1024 * 1024),
        cost_estimate=pl.CostEstimate(
            flops=2 * rows * width * f * 4,
            transcendentals=0,
            bytes_accessed=2 * (3 * rows * width + 4 * width * f + rows * 4 * f),
        ),
    )(both, both, inverse.reshape(rows, 1), gain.reshape(1, width), w_gate, w_up, probe, w_down)


def second_kernel(s_ref, o_ref):
    f = o_ref.shape[2]
    x = s_ref[0].astype(jnp.float32)
    second = second_factor(x[:, :f], x[:, f:2 * f], x[:, 2 * f:3 * f], x[:, 3 * f:])
    for j in range(o_ref.shape[0]):
        o_ref[j] = second


def second_repeated(summed, copies):
    rows, f = summed.shape[1], summed.shape[2] // 4
    return pl.pallas_call(
        second_kernel,
        out_shape=jax.ShapeDtypeStruct((copies, rows, f), jnp.bfloat16),
        in_specs=[pl.BlockSpec(memory_space=pltpu.VMEM)],
        out_specs=pl.BlockSpec(memory_space=pltpu.VMEM),
    )(summed)


def gather_tensor(x, axis):
    n = lax.axis_size(axis)
    repeated = jnp.broadcast_to(x[None], (n,) + x.shape)
    got = lax.all_to_all(repeated, axis, 0, 0, tiled=True)
    return got.reshape((n * x.shape[0],) + x.shape[1:])


def butterfly_sum(x, axis):
    n = lax.axis_size(axis)
    bit = 1
    while bit < n:
        x = x + lax.ppermute(x, axis, [(i, i ^ bit) for i in range(n)])
        bit *= 2
    return x


def body(tokens, cotangent, gain, w_gate, w_up, w_down, probe):
    n_tensor = lax.axis_size("tensor")
    width = tokens.shape[1]
    both = lax.all_gather(jnp.concatenate([tokens, cotangent], axis=1), "seq", axis=0, tiled=True)
    values = tokens.astype(jnp.float32)
    squares = butterfly_sum(jnp.sum(values * values, axis=1), "tensor")
    inverse = gather_tensor(lax.rsqrt(squares / D + epsilon), "seq")
    total_tokens = both.shape[0]
    unit_count = w_gate.shape[1]
    parts, normed = products(both, inverse, gain, w_gate, w_up, probe, w_down, n_tensor)
    summed = lax.psum_scatter(parts, "tensor", scatter_dimension=0, tiled=True)
    repeated = second_repeated(summed, n_tensor)
    gathered = lax.all_to_all(repeated, "tensor", 0, 0, tiled=True)
    product = lax.dot_general(
        normed,
        gathered.reshape(-1, unit_count),
        (((0,), (0,)), ((), ())),
        preferred_element_type=jnp.float32,
    )
    return product / total_tokens


def solution(mesh):
    return jax.shard_map(
        body,
        mesh=mesh,
        in_specs=(
            P("seq", "tensor"),
            P("seq", "tensor"),
            P("tensor"),
            P("tensor", "seq"),
            P("tensor", "seq"),
            P("seq", "tensor"),
            P("tensor", "seq"),
        ),
        out_specs=P("tensor", "seq"),
        check_vma=False,
    )
```

```python
import functools

import jax
import jax.numpy as jnp
from jax import lax
from jax.experimental import pallas as pl
from jax.experimental.pallas import tpu as pltpu
from jax.sharding import PartitionSpec as P

D = 8192

epsilon = 1e-05


def second_factor(pre_gate, pre_up, tangent, upstream):
    sigmoid_gate = jax.nn.sigmoid(pre_gate)
    curvature = sigmoid_gate * (1.0 - sigmoid_gate) * (2.0 + pre_gate * (1.0 - 2.0 * sigmoid_gate))
    return (upstream * pre_up * curvature * tangent).astype(jnp.bfloat16)


def products_kernel(t_ref, c_ref, inv_ref, gain_ref, wg_ref, wu_ref, pr_ref, wd_ref, o_ref, n_out_ref):
    f = wg_ref.shape[1]
    n = (t_ref[...].astype(jnp.float32) * inv_ref[...] * gain_ref[...]).astype(jnp.bfloat16)
    n_out_ref[...] = n
    for p, w_ref in enumerate((wg_ref, wu_ref, pr_ref)):
        o_ref[0, :, p * f:(p + 1) * f] = jnp.dot(
            n, w_ref[...], preferred_element_type=jnp.float32
        ).astype(o_ref.dtype)
    o_ref[0, :, 3 * f:4 * f] = lax.dot_general(
        c_ref[...], wd_ref[...], (((1,), (1,)), ((), ())), preferred_element_type=jnp.float32
    ).astype(o_ref.dtype)


def products(both, inverse, gain, w_gate, w_up, probe, w_down, blocks):
    rows, width = both.shape[0], both.shape[1] // 2
    f = w_gate.shape[1]
    tm = rows // blocks
    full = lambda shape: pl.BlockSpec(shape, lambda i: (0, 0))
    return pl.pallas_call(
        products_kernel,
        out_shape=(
            jax.ShapeDtypeStruct((blocks, tm, 4 * f), jnp.bfloat16),
            jax.ShapeDtypeStruct((rows, width), jnp.bfloat16),
        ),
        grid=(blocks,),
        in_specs=[
            pl.BlockSpec((tm, width), lambda i: (i, 0)),
            pl.BlockSpec((tm, width), lambda i: (i, 1)),
            pl.BlockSpec((tm, 1), lambda i: (i, 0)),
            full((1, width)),
            full(w_gate.shape),
            full(w_up.shape),
            full(probe.shape),
            full(w_down.shape),
        ],
        out_specs=(
            pl.BlockSpec((1, tm, 4 * f), lambda i: (i, 0, 0)),
            pl.BlockSpec((tm, width), lambda i: (i, 0)),
        ),
        cost_estimate=pl.CostEstimate(
            flops=2 * rows * width * f * 4,
            transcendentals=0,
            bytes_accessed=2 * (3 * rows * width + 4 * width * f + rows * 4 * f),
        ),
    )(both, both, inverse.reshape(rows, 1), gain.reshape(1, width), w_gate, w_up, probe, w_down)


def gather_tensor(x, axis):
    n = lax.axis_size(axis)
    repeated = jnp.broadcast_to(x[None], (n,) + x.shape)
    got = lax.all_to_all(repeated, axis, 0, 0, tiled=True)
    return got.reshape((n * x.shape[0],) + x.shape[1:])


def butterfly_sum(x, axis):
    n = lax.axis_size(axis)
    bit = 1
    while bit < n:
        x = x + lax.ppermute(x, axis, [(i, i ^ bit) for i in range(n)])
        bit *= 2
    return x


def body(tokens, cotangent, gain, w_gate, w_up, w_down, probe):
    n_tensor = lax.axis_size("tensor")
    width = tokens.shape[1]
    both = lax.all_gather(jnp.concatenate([tokens, cotangent], axis=1), "seq", axis=0, tiled=True)
    values = tokens.astype(jnp.float32)
    squares = butterfly_sum(jnp.sum(values * values, axis=1), "tensor")
    inverse = gather_tensor(lax.rsqrt(squares / D + epsilon), "seq")
    total_tokens = both.shape[0]
    unit_count = w_gate.shape[1]
    parts, normed = products(both, inverse, gain, w_gate, w_up, probe, w_down, n_tensor)
    summed = lax.psum_scatter(parts, "tensor", scatter_dimension=0, tiled=True)[0].astype(jnp.float32)
    second = second_factor(
        summed[:, :unit_count],
        summed[:, unit_count : 2 * unit_count],
        summed[:, 2 * unit_count : 3 * unit_count],
        summed[:, 3 * unit_count :],
    )
    product = lax.dot_general(
        normed,
        gather_tensor(second, "tensor"),
        (((0,), (0,)), ((), ())),
        preferred_element_type=jnp.float32,
    )
    return product / total_tokens


def solution(mesh):
    return jax.shard_map(
        body,
        mesh=mesh,
        in_specs=(
            P("seq", "tensor"),
            P("seq", "tensor"),
            P("tensor"),
            P("tensor", "seq"),
            P("tensor", "seq"),
            P("seq", "tensor"),
            P("tensor", "seq"),
        ),
        out_specs=P("tensor", "seq"),
        check_vma=False,
    )
```

```python
import functools

import jax
import jax.numpy as jnp
from jax import lax
from jax.experimental import pallas as pl
from jax.experimental.pallas import tpu as pltpu
from jax.sharding import PartitionSpec as P

D = 8192

epsilon = 1e-05


def second_factor(pre_gate, pre_up, tangent, upstream):
    sigmoid_gate = jax.nn.sigmoid(pre_gate)
    curvature = sigmoid_gate * (1.0 - sigmoid_gate) * (2.0 + pre_gate * (1.0 - 2.0 * sigmoid_gate))
    return (upstream * pre_up * curvature * tangent).astype(jnp.bfloat16)


def products_kernel(t_ref, c_ref, inv_ref, gain_ref, wg_ref, wu_ref, pr_ref, wd_ref, o_ref, n_out_ref):
    f = wg_ref.shape[1]
    rows = n_out_ref.shape[0]
    t = t_ref[...].reshape(rows, t_ref.shape[-1])
    n = (t.astype(jnp.float32) * inv_ref[...] * gain_ref[...]).astype(jnp.bfloat16)
    n_out_ref[...] = n
    for p, w_ref in enumerate((wg_ref, wu_ref, pr_ref)):
        o_ref[0, :, p * f:(p + 1) * f] = jnp.dot(
            n, w_ref[...], preferred_element_type=jnp.float32
        ).astype(o_ref.dtype)
    o_ref[0, :, 3 * f:4 * f] = lax.dot_general(
        c_ref[...].reshape(rows, c_ref.shape[-1]), wd_ref[...], (((1,), (1,)), ((), ())),
        preferred_element_type=jnp.float32
    ).astype(o_ref.dtype)


def products(both, inverse, gain, w_gate, w_up, probe, w_down, blocks):
    seqs, _, local, width = both.shape
    rows = seqs * local
    f = w_gate.shape[1]
    tm = rows // blocks
    per = tm // local
    full = lambda shape: pl.BlockSpec(shape, lambda i: (0, 0))
    return pl.pallas_call(
        products_kernel,
        out_shape=(
            jax.ShapeDtypeStruct((blocks, tm, 4 * f), jnp.bfloat16),
            jax.ShapeDtypeStruct((rows, width), jnp.bfloat16),
        ),
        grid=(blocks,),
        in_specs=[
            pl.BlockSpec((per, 1, local, width), lambda i: (i, 0, 0, 0)),
            pl.BlockSpec((per, 1, local, width), lambda i: (i, 1, 0, 0)),
            pl.BlockSpec((tm, 1), lambda i: (i, 0)),
            full((1, width)),
            full(w_gate.shape),
            full(w_up.shape),
            full(probe.shape),
            full(w_down.shape),
        ],
        out_specs=(
            pl.BlockSpec((1, tm, 4 * f), lambda i: (i, 0, 0)),
            pl.BlockSpec((tm, width), lambda i: (i, 0)),
        ),
        cost_estimate=pl.CostEstimate(
            flops=2 * rows * width * f * 4,
            transcendentals=0,
            bytes_accessed=2 * (3 * rows * width + 4 * width * f + rows * 4 * f),
        ),
    )(both, both, inverse.reshape(rows, 1), gain.reshape(1, width), w_gate, w_up, probe, w_down)


def gather_tensor(x, axis):
    n = lax.axis_size(axis)
    repeated = jnp.broadcast_to(x[None], (n,) + x.shape)
    got = lax.all_to_all(repeated, axis, 0, 0, tiled=True)
    return got.reshape((n * x.shape[0],) + x.shape[1:])


def butterfly_sum(x, axis):
    n = lax.axis_size(axis)
    bit = 1
    while bit < n:
        x = x + lax.ppermute(x, axis, [(i, i ^ bit) for i in range(n)])
        bit *= 2
    return x


def body(tokens, cotangent, gain, w_gate, w_up, w_down, probe):
    n_tensor = lax.axis_size("tensor")
    width = tokens.shape[1]
    local_rows = tokens.shape[0]
    both = lax.all_gather(jnp.concatenate([tokens, cotangent], axis=0), "seq", axis=0, tiled=True)
    both = both.reshape(-1, 2, local_rows, width)
    values = tokens.astype(jnp.float32)
    squares = butterfly_sum(jnp.sum(values * values, axis=1), "tensor")
    inverse = gather_tensor(lax.rsqrt(squares / D + epsilon), "seq")
    total_tokens = both.shape[0] * local_rows
    unit_count = w_gate.shape[1]
    parts, normed = products(both, inverse, gain, w_gate, w_up, probe, w_down, n_tensor)
    summed = lax.psum_scatter(parts, "tensor", scatter_dimension=0, tiled=True)[0].astype(jnp.float32)
    second = second_factor(
        summed[:, :unit_count],
        summed[:, unit_count : 2 * unit_count],
        summed[:, 2 * unit_count : 3 * unit_count],
        summed[:, 3 * unit_count :],
    )
    product = lax.dot_general(
        normed,
        gather_tensor(second, "tensor"),
        (((0,), (0,)), ((), ())),
        preferred_element_type=jnp.float32,
    )
    return product / total_tokens


def solution(mesh):
    return jax.shard_map(
        body,
        mesh=mesh,
        in_specs=(
            P("seq", "tensor"),
            P("seq", "tensor"),
            P("tensor"),
            P("tensor", "seq"),
            P("tensor", "seq"),
            P("seq", "tensor"),
            P("tensor", "seq"),
        ),
        out_specs=P("tensor", "seq"),
        check_vma=False,
    )
```
